32 devices in a mesh: tile: 8 (over z, y), view: 4 (over x, core).
Axes of the slice: x: 2, y: 2, z: 4, core: 2. Of those that a mesh axis runs over, the one named last changes fastest.
Arguments:
- recorded: bfloat16 [4, 128, 256, 256], P('view', 'tile'), may hold values from 0.099609375 to 10
- estimate: float32 [128, 256, 256], P('tile', 'view'), may hold values from 0.5 to 2
- psf_taps: float32 [16, 3, 31], replicated, may hold values from 0.05 to 1
- half_width: int32 [16, 3], replicated, may hold values from 8 to 15
- assign: int32 [4], replicated, may hold values from 0 to 15
- flags: int32 [16, 32], P('tile', 'view'), may hold values 0 or 1
Outputs:
- restored: float32 [128, 256, 256], P('tile', 'view')
The draws below stay inside these ranges and needn't reach their ends.
All inputs are finite; a program needn't handle non-finite values. No bound on the sum of `flags` on one device may be relied on, other than what follows from the above.
Results may differ from the reference program's by a relative error of at most 0.0007.
Values may be sent and summed in bfloat16 or wider, within the bound.
A program may use at most 64 MiB of HBM per device.

```python
import math
import jax
import jax.numpy as jnp
from jax import lax

NY = 256
NZ = 256
VIEWS = 4
KERNELS = 16
TAPS = 31
ITERS = 1
NX = 128


def plant(entries, rng, least, top_value):
    extent = entries.shape
    spot = [jax.random.randint(jax.random.fold_in(rng, axis), (), 0, extent[axis]) for axis in range(len(extent))]
    entries = entries.at[tuple(spot)].set(least)
    longest = extent.index(max(extent))
    spot[longest] = (spot[longest] + 1) % extent[longest]
    return entries.at[tuple(spot)].set(top_value)


def block_scale(stream_key, shape, shards, low, top_value):
    level, own = 1.0, jax.random.fold_in(stream_key, 6)
    for axis_at, shards_of in shards:
        steps = jnp.exp(jax.random.uniform(jax.random.fold_in(own, axis_at), (shards_of,), jnp.float32, low / len(shards), top_value / len(shards)))
        level = level * jnp.repeat(steps, shape[axis_at] // shards_of).reshape([-1 if axis == axis_at else 1 for axis in range(len(shape))])
    return level


def setup_inputs(seed: int = 0) -> dict:
    splits = jax.random.split(jax.random.key(seed), 7)
    return {
        "recorded": jnp.clip(jnp.exp(math.log(10.0) - 4.609084 * jax.random.uniform(splits[0], (VIEWS, NX, NY, NZ), jnp.float32) ** block_scale(splits[0], (VIEWS, NX, NY, NZ), ((0, 4), (1, 8)), -0.2, 0.2)), 0.099609375, 10.0).astype(jnp.bfloat16),
        "estimate": jnp.clip(jnp.exp(math.log(2.0) - 1.3862944 * jax.random.uniform(splits[1], (NX, NY, NZ), jnp.float32) ** block_scale(splits[1], (NX, NY, NZ), ((0, 8), (1, 4)), -0.2, 0.2)), 0.5, 2.0),
        "psf_taps": jnp.clip(jnp.exp(jax.random.uniform(splits[2], (KERNELS, 3, TAPS), jnp.float32, math.log(0.05), math.log(1.0))), 0.05, 1.0),
        "half_width": plant(jax.random.randint(splits[3], (KERNELS, 3), 8, 16), jax.random.fold_in(splits[3], 1), 8, 15).astype(jnp.int32),
        "assign": plant(jax.random.randint(splits[4], (VIEWS,), 0, KERNELS), jax.random.fold_in(splits[4], 1), 0, KERNELS - 1).astype(jnp.int32),
        "flags": plant((jax.random.randint(splits[5], (NX // 8, NY // 8), 0, 4) < 3).astype(jnp.int32), jax.random.fold_in(splits[5], 1), 0, 1),
    }


def make_kernels(psf_taps, half_width, assign):
    offsets = jnp.abs(jnp.arange(TAPS) - TAPS // 2)
    keep = (offsets[None, None, :] <= half_width[:, :, None]).astype(jnp.float32)
    raw = psf_taps * keep
    kern = raw / jnp.sum(raw, axis=-1, keepdims=True)
    picker = (assign[:, None] == jnp.arange(KERNELS)[None, :]).astype(jnp.float32)
    return jnp.einsum("sv,vaj->saj", picker, kern, precision=lax.Precision.HIGHEST)


def band_matrix(kernel, length):
    rows = jnp.arange(length)[:, None]
    cols = jnp.arange(length)[None, :]
    offset = rows - cols + TAPS // 2
    hits = (offset[None, :, :] == jnp.arange(TAPS)[:, None, None]).astype(jnp.float32)
    return jnp.sum(kernel[:, None, None] * hits, axis=0)


def blur_three(volume, kernels):
    padded = jnp.pad(volume, ((TAPS // 2, TAPS // 2), (0, 0), (0, 0)))
    length = volume.shape[0]
    along = jnp.zeros_like(volume)
    for j in range(TAPS):
        along = along + kernels[0, j] * padded[j:j + length]
    along = jnp.einsum("xpz,pi->xiz", along, band_matrix(kernels[1], volume.shape[1]), precision=lax.Precision.HIGHEST)
    return jnp.einsum("xyp,pi->xyi", along, band_matrix(kernels[2], volume.shape[2]), precision=lax.Precision.HIGHEST)


def reference(recorded, estimate, psf_taps, half_width, assign, flags):
    kernels = make_kernels(psf_taps, half_width, assign)
    flipped = kernels[:, :, ::-1]
    cells = jnp.repeat(jnp.repeat(flags, 8, axis=0), 8, axis=1)[:, :, None] > 0
    current = estimate
    for step in range(ITERS):
        rounded = lax.optimization_barrier(current.astype(jnp.bfloat16)).astype(jnp.float32)

        def one_slot(total, items):
            slot_data, slot_kern, slot_flip = items
            blurred = blur_three(rounded, slot_kern)
            ratio = (slot_data.astype(jnp.float32) / blurred).astype(jnp.bfloat16)
            ratio = lax.optimization_barrier(ratio).astype(jnp.float32)
            return total + blur_three(ratio, slot_flip), None

        total, _ = lax.scan(one_slot, jnp.zeros_like(current), (recorded, kernels, flipped))
        correction = total / VIEWS
        current = jnp.where(cells, current * correction, current)
    return current
```

```python
import jax
import jax.numpy as jnp
from jax import lax
from jax.sharding import PartitionSpec as P

VIEWS = 4
KERNELS = 16
TAPS = 31
HALF = TAPS // 2
HIGH = lax.Precision.HIGH


def make_kernels(psf_taps, half_width, assign):
    offsets = jnp.abs(jnp.arange(TAPS) - HALF)
    keep = (offsets[None, None, :] <= half_width[:, :, None]).astype(jnp.float32)
    raw = psf_taps * keep
    kern = raw / jnp.sum(raw, axis=-1, keepdims=True)
    picker = (assign[:, None] == jnp.arange(KERNELS)[None, :]).astype(jnp.float32)
    return jnp.einsum("sv,vaj->saj", picker, kern, precision=lax.Precision.HIGHEST)


def band_matrix(kernel, rows_count, cols_count, shift):
    rows = jnp.arange(rows_count)[:, None]
    cols = jnp.arange(cols_count)[None, :]
    offset = rows - cols + shift
    hits = (offset[None, :, :] == jnp.arange(TAPS)[:, None, None]).astype(jnp.float32)
    return jnp.sum(kernel[:, None, None] * hits, axis=0)


def shards(recorded, estimate, psf_taps, half_width, assign, flags):
    slab = estimate.shape[0]
    full_y = recorded.shape[2]
    depth_z = recorded.shape[3]
    count = lax.axis_size("tile")
    up = [(i, i + 1) for i in range(count - 1)]
    down = [(i + 1, i) for i in range(count - 1)]
    kernels = make_kernels(psf_taps, half_width, assign)
    slot = lax.axis_index("view")
    selector = (jnp.arange(VIEWS) == slot).astype(jnp.float32)
    own_kern = jnp.einsum("s,saj->aj", selector, kernels, precision=lax.Precision.HIGHEST)
    second_own = band_matrix(own_kern[1], full_y, full_y, HALF)
    third_own = band_matrix(own_kern[2], depth_z, depth_z, HALF)
    padded_rows = slab + TAPS - 1
    first_all = jnp.stack([band_matrix(kernels[s, 0], padded_rows, slab, 0) for s in range(VIEWS)])
    cells = jnp.repeat(jnp.repeat(flags, 8, axis=0), 8, axis=1)[:, :, None] > 0
    rounded = estimate.astype(jnp.bfloat16)
    padded = jnp.concatenate(
        [
            lax.ppermute(rounded[slab - HALF:], "tile", up),
            rounded,
            lax.ppermute(rounded[:HALF], "tile", down),
        ],
        axis=0,
    ).astype(jnp.float32)
    stacked = jnp.einsum("pyz,spi->siyz", padded, first_all, precision=HIGH)
    first_pass = lax.all_to_all(
        stacked.astype(jnp.bfloat16), "view", split_axis=0, concat_axis=2, tiled=True
    )[0].astype(jnp.float32)
    blurred = jnp.einsum("xpz,pi->xiz", first_pass, second_own, precision=HIGH)
    blurred = jnp.einsum("xyp,pi->xyi", blurred, third_own, precision=HIGH)
    ratio = (recorded[0].astype(jnp.float32) / blurred).astype(jnp.bfloat16).astype(jnp.float32)
    back = jnp.einsum("xpz,ip->xiz", ratio, second_own, precision=HIGH)
    back = jnp.einsum("xyp,ip->xyi", back, third_own, precision=HIGH)
    parts = lax.all_to_all(
        back.astype(jnp.bfloat16)[None], "view", split_axis=2, concat_axis=0, tiled=True
    ).astype(jnp.float32)
    wide = jnp.einsum("spyz,sip->iyz", parts, first_all, precision=HIGH)
    spread = wide.astype(jnp.bfloat16)
    below = lax.ppermute(spread[slab + HALF:], "tile", up).astype(jnp.float32)
    above = lax.ppermute(spread[:HALF], "tile", down).astype(jnp.float32)
    total = wide[HALF:slab + HALF]
    total = total + jnp.pad(below, ((0, slab - HALF), (0, 0), (0, 0)))
    total = total + jnp.pad(above, ((slab - HALF, 0), (0, 0), (0, 0)))
    correction = total / VIEWS
    return jnp.where(cells, estimate * correction, estimate)


def solution(mesh):
    placed = (
        P("view", "tile", None, None),
        P("tile", "view", None),
        P(),
        P(),
        P(),
        P("tile", "view"),
    )
    return jax.shard_map(
        shards, mesh=mesh, in_specs=placed, out_specs=P("tile", "view", None), check_vma=False
    )
```

```python
import functools

import jax
import jax.numpy as jnp
from jax import lax
from jax.experimental import pallas as pl
from jax.experimental.pallas import tpu as pltpu
from jax.sharding import PartitionSpec as P

TAPS = 31
HALF = TAPS // 2
GROUP = 8
CHUNK = 16
F32 = jnp.float32
BF16 = jnp.bfloat16
MESH = pl.DeviceIdType.MESH


def dot(a, b):
    return jnp.dot(a, b, preferred_element_type=F32)


def dot_nt(a, b):
    return lax.dot_general(a, b, (((1,), (1,)), ((), ())), preferred_element_type=F32)


def picked_taps(entry, half_ref, psf_ref, taps):
    taps[0:3, 0:TAPS] = psf_ref[entry]
    row = lax.broadcasted_iota(jnp.int32, taps.shape, 0)
    col = lax.broadcasted_iota(jnp.int32, taps.shape, 1)
    width = jnp.where(
        row == 0, half_ref[entry, 0], jnp.where(row == 1, half_ref[entry, 1], half_ref[entry, 2])
    )
    keep = (jnp.abs(col - HALF) <= width) & (col < TAPS) & (row < 3)
    return jnp.where(keep, taps[...], 0.0).astype(BF16).astype(F32)


def band(line, size):
    rolled = pltpu.roll(
        jnp.broadcast_to(line, (size, size)), size - HALF, 1, stride=1, stride_axis=0
    )
    row = lax.broadcasted_iota(jnp.int32, (size, size), 0)
    col = lax.broadcasted_iota(jnp.int32, (size, size), 1)
    return jnp.where(jnp.abs(row - col) <= HALF, rolled, 0.0)


def kernel(
    assign_ref, half_ref, psf_ref, rounded, recorded_hbm, out,
    taps, wide_a, wide_b, cy, cyt, cz, recorded,
    from_low, from_high, mixed, first, second, sent, parts,
    to_low, to_high, back_low, back_high,
    rec_sem, halo_send, halo_recv, mix_send, mix_recv,
    part_send, part_recv, sum_send, sum_recv,
):
    views = parts.shape[0]
    slab, quarter, depth = rounded.shape
    chunks = quarter // CHUNK
    tile, view = lax.axis_index("tile"), lax.axis_index("view")
    last = lax.axis_size("tile") - 1
    has_low, has_high = tile > 0, tile < last

    def ys(c, base=0):
        return pl.ds(pl.multiple_of(base + c * CHUNK, CHUNK), CHUNK)

    def peer(k):
        return lax.rem(view + k, views)

    def remote(src, dst, send, recv, device):
        return pltpu.make_async_remote_copy(
            src_ref=src, dst_ref=dst, send_sem=send, recv_sem=recv,
            device_id=device, device_id_type=MESH,
        )

    def halo_up(c):
        return remote(
            rounded.at[slab - HALF:slab, ys(c)], from_low.at[slab - HALF:slab, ys(c)],
            halo_send.at[0, c], halo_recv.at[0, c], {"tile": tile + 1},
        )

    def halo_down(c):
        return remote(
            rounded.at[0:HALF, ys(c)], from_high.at[0:HALF, ys(c)],
            halo_send.at[1, c], halo_recv.at[1, c], {"tile": tile - 1},
        )

    def mix(k, c):
        return remote(
            mixed.at[peer(k), :, ys(c)], first.at[:, ys(c, view * quarter)],
            mix_send.at[k - 1, c], mix_recv.at[k - 1, c], {"view": peer(k)},
        )

    def part(k, c):
        return remote(
            sent.at[k - 1, :, ys(c)], parts.at[view, :, ys(c)],
            part_send.at[k - 1, c], part_recv.at[k - 1, c], {"view": peer(k)},
        )

    def sum_up(c):
        return remote(
            to_high.at[:, ys(c)], back_low.at[:, ys(c)],
            sum_send.at[0, c], sum_recv.at[0, c], {"tile": tile + 1},
        )

    def sum_down(c):
        return remote(
            to_low.at[:, ys(c)], back_high.at[:, ys(c)],
            sum_send.at[1, c], sum_recv.at[1, c], {"tile": tile - 1},
        )

    def each_chunk(body):
        def step(c, carry):
            body(c)
            return carry
        lax.fori_loop(0, chunks, step, 0)

    rec_copy = pltpu.make_async_copy(recorded_hbm.at[0], recorded, rec_sem)
    rec_copy.start()
    for ref in (from_low, from_high, back_low, back_high):
        ref[...] = jnp.zeros_like(ref)
    barrier = pltpu.get_barrier_semaphore()
    for k in range(1, views):
        pl.semaphore_signal(barrier, inc=1, device_id={"view": peer(k)}, device_id_type=MESH)

    @pl.when(has_low)
    def _():
        pl.semaphore_signal(barrier, inc=1, device_id={"tile": tile - 1}, device_id_type=MESH)

    @pl.when(has_high)
    def _():
        pl.semaphore_signal(barrier, inc=1, device_id={"tile": tile + 1}, device_id_type=MESH)

    pl.semaphore_wait(
        barrier, views - 1 + has_low.astype(jnp.int32) + has_high.astype(jnp.int32)
    )

    def start_halo(c):
        @pl.when(has_high)
        def _():
            halo_up(c).start()

        @pl.when(has_low)
        def _():
            halo_down(c).start()

    each_chunk(start_halo)

    taps[...] = jnp.zeros_like(taps)
    rows, cols = slab * GROUP, 3 * slab * GROUP
    tap = lax.broadcasted_iota(jnp.int32, (taps.shape[1], cols), 0)
    spot = lax.broadcasted_iota(jnp.int32, (taps.shape[1], cols), 1)
    spread = ((spot == GROUP * (tap + slab - HALF)) & (tap < TAPS)).astype(F32).astype(BF16)
    for s in range(views):
        lines = picked_taps(assign_ref[s], half_ref, psf_ref, taps)
        line = dot(lines.astype(BF16), spread)[0:1]
        block = pltpu.roll(jnp.broadcast_to(line, (rows, cols)), 0, 1, stride=1, stride_axis=0)
        wide_a[s * rows:(s + 1) * rows, :] = block.astype(BF16)
        wide_b[:, s * rows:(s + 1) * rows] = block.T.astype(BF16)
    lines = picked_taps(assign_ref[view], half_ref, psf_ref, taps)
    totals = jnp.sum(lines, axis=1, keepdims=True)
    scale = 1.0 / (totals[0:1] * totals[1:2] * totals[2:3])
    across = band(lines[1:2], cy.shape[0])
    cy[...] = across.astype(BF16)
    cyt[...] = across.T.astype(BF16)
    cz[...] = band(lines[2:3], depth).astype(BF16)

    def blur_first(c):
        @pl.when(has_low)
        def _():
            halo_up(c).wait_recv()

        @pl.when(has_high)
        def _():
            halo_down(c).wait_recv()

        cells = jnp.concatenate(
            [from_low[:, ys(c), :], rounded[:, ys(c), :], from_high[:, ys(c), :]], axis=0
        ).astype(F32)
        halves = []
        for h in range(0, CHUNK, GROUP):
            some = cells[:, h:h + GROUP, :].reshape(cols, depth).astype(BF16)
            halves.append(dot(wide_a[...], some).reshape(views * slab, GROUP, depth))
        mixed[:, :, ys(c), :] = (
            jnp.concatenate(halves, axis=1).astype(BF16).reshape(views, slab, CHUNK, depth)
        )
        for k in range(1, views):
            mix(k, c).start()
        first[:, ys(c, view * quarter), :] = mixed[view, :, ys(c), :]

    each_chunk(blur_first)

    def wait_mix(c):
        for k in range(1, views):
            mix(k, c).wait_recv()

    each_chunk(wait_mix)
    rec_copy.wait()

    def plane(i, carry):
        blurred = dot(cy[...], first[i]).astype(BF16)
        blurred = dot_nt(blurred, cz[...]) * scale
        ratio = (recorded[i].astype(F32) / blurred).astype(BF16)
        second[i] = dot(cyt[...], ratio).astype(BF16)
        return carry

    lax.fori_loop(0, slab, plane, 0)

    def spread_parts(c):
        for k in list(range(1, views)) + [0]:
            lines = second[:, ys(c, peer(k) * quarter), :].reshape(slab * CHUNK, depth)
            value = (dot(lines, cz[...]) * scale).astype(BF16).reshape(slab, CHUNK, depth)
            if k:
                sent[k - 1, :, ys(c), :] = value
                part(k, c).start()
            else:
                parts[view, :, ys(c), :] = value

    each_chunk(spread_parts)

    def blur_last(c):
        for k in range(1, views):
            part(k, c).wait_recv()
        cells = parts[:, :, ys(c), :].astype(F32).reshape(views * slab, CHUNK, depth)
        halves = []
        for h in range(0, CHUNK, GROUP):
            some = cells[:, h:h + GROUP, :].reshape(views * rows, depth).astype(BF16)
            halves.append(dot(wide_b[...], some).reshape(3 * slab, GROUP, depth))
        wide = jnp.concatenate(halves, axis=1)
        out[:, ys(c), :] = wide[slab:2 * slab]
        for block, target, spare in (
            (wide[:slab], to_low, 0), (wide[2 * slab:], to_high, slab - 1)
        ):
            mean = (jnp.sum(block, axis=1) * (1.0 / CHUNK)).astype(BF16)
            target[:, ys(c), :] = (block - mean.astype(F32)[:, None, :]).astype(BF16)
            target[spare, ys(c), :] = mean

        @pl.when(has_high)
        def _():
            sum_up(c).start()

        @pl.when(has_low)
        def _():
            sum_down(c).start()

    each_chunk(blur_last)

    def add_sums(c):
        @pl.when(has_low)
        def _():
            sum_up(c).wait_recv()

        @pl.when(has_high)
        def _():
            sum_down(c).wait_recv()

        for came, spare in ((back_low, slab - 1), (back_high, 0)):
            mean = came[spare, ys(c), :].astype(F32)[:, None, :]
            added = came[:, ys(c), :].astype(F32) + mean
            for i in range(slab):
                if i != spare:
                    out[i, ys(c), :] += added[i]

    each_chunk(add_sums)

    def wait_sends(c):
        for k in range(1, views):
            mix(k, c).wait_send()
            part(k, c).wait_send()

        @pl.when(has_high)
        def _():
            halo_up(c).wait_send()
            sum_up(c).wait_send()

        @pl.when(has_low)
        def _():
            halo_down(c).wait_send()
            sum_down(c).wait_send()

    each_chunk(wait_sends)


def shards(recorded, estimate, psf_taps, half_width, assign, flags):
    views = lax.axis_size("view")
    slab, quarter, depth = estimate.shape
    full_y = recorded.shape[2]
    chunks = quarter // CHUNK
    rows, cols = slab * GROUP, 3 * slab * GROUP
    cells = jnp.repeat(jnp.repeat(flags, 8, axis=0), 8, axis=1)[:, :, None] > 0
    vmem = pl.BlockSpec(memory_space=pltpu.VMEM)
    smem = pl.BlockSpec(memory_space=pltpu.SMEM)
    dma = pltpu.SemaphoreType.DMA
    edge = pltpu.VMEM((slab, quarter, depth), BF16)
    whole = pltpu.VMEM((slab, full_y, depth), BF16)
    total = pl.pallas_call(
        kernel,
        out_shape=jax.ShapeDtypeStruct(estimate.shape, F32),
        in_specs=[smem, smem, vmem, vmem, pl.BlockSpec(memory_space=pl.ANY)],
        out_specs=vmem,
        scratch_shapes=[
            pltpu.VMEM((8, 256), F32),
            pltpu.VMEM((views * rows, cols), BF16),
            pltpu.VMEM((cols, views * rows), BF16),
            pltpu.VMEM((full_y, full_y), BF16),
            pltpu.VMEM((full_y, full_y), BF16),
            pltpu.VMEM((depth, depth), BF16),
            whole,
            edge, edge,
            pltpu.VMEM((views, slab, quarter, depth), BF16),
            whole, whole,
            pltpu.VMEM((views - 1, slab, quarter, depth), BF16),
            pltpu.VMEM((views, slab, quarter, depth), BF16),
            edge, edge, edge, edge,
            dma,
            dma((2, chunks)), dma((2, chunks)),
            dma((views - 1, chunks)), dma((views - 1, chunks)),
            dma((views - 1, chunks)), dma((views - 1, chunks)),
            dma((2, chunks)), dma((2, chunks)),
        ],
        compiler_params=pltpu.CompilerParams(collective_id=0, has_side_effects=True),
        name="deconvolve",
    )(assign, half_width, psf_taps, estimate.astype(BF16), recorded)
    return jnp.where(cells, estimate * (total / views), estimate)


def solution(mesh):
    placed = (
        P("view", "tile", None, None),
        P("tile", "view", None),
        P(),
        P(),
        P(),
        P("tile", "view"),
    )
    return jax.shard_map(
        shards, mesh=mesh, in_specs=placed, out_specs=P("tile", "view", None), check_vma=False
    )
```

```python
import jax
import jax.numpy as jnp
from jax import lax
from jax.experimental import pallas as pl
from jax.experimental.pallas import tpu as pltpu
from jax.sharding import PartitionSpec as P

TAPS = 31
HALF = TAPS // 2
GROUP = 8
CHUNK = 16
PLANES = 4
F32 = jnp.float32
BF16 = jnp.bfloat16
MESH = pl.DeviceIdType.MESH


def dot(a, b):
    return jnp.dot(a, b, preferred_element_type=F32)


def dot_nt(a, b):
    return lax.dot_general(a, b, (((1,), (1,)), ((), ())), preferred_element_type=F32)


def picked_taps(entry, half_ref, psf_ref, taps):
    for d in range(3):
        taps[d:d + 1, 0:TAPS] = psf_ref[d, pl.ds(entry, 1), :]
    row = lax.broadcasted_iota(jnp.int32, taps.shape, 0)
    col = lax.broadcasted_iota(jnp.int32, taps.shape, 1)
    width = jnp.where(
        row == 0, half_ref[0, entry], jnp.where(row == 1, half_ref[1, entry], half_ref[2, entry])
    )
    keep = (jnp.abs(col - HALF) <= width) & (col < TAPS) & (row < 3)
    return jnp.where(keep, taps[...], 0.0).astype(BF16).astype(F32)


def band(line, size):
    rolled = pltpu.roll(
        jnp.broadcast_to(line, (size, size)), size - HALF, 1, stride=1, stride_axis=0
    )
    row = lax.broadcasted_iota(jnp.int32, (size, size), 0)
    col = lax.broadcasted_iota(jnp.int32, (size, size), 1)
    return jnp.where(jnp.abs(row - col) <= HALF, rolled, 0.0)


def kernel(
    assign_ref, half_ref, psf_ref, rounded, recorded_hbm, out,
    taps, wide_a, wide_b, cy, cyt, cz, recorded,
    from_low, from_high, mixed, first, second, parts,
    to_low, to_high, back_low, back_high,
    rec_sem, halo_send, halo_recv, mix_send, mix_recv,
    part_send, part_recv, early_send, early_recv, sum_send, sum_recv,
):
    views = parts.shape[0]
    slab, quarter, depth = rounded.shape
    chunks = quarter // CHUNK
    tile, view = lax.axis_index("tile"), lax.axis_index("view")
    last = lax.axis_size("tile") - 1
    has_low, has_high = tile > 0, tile < last

    def ys(c, base=0):
        return pl.ds(pl.multiple_of(base + c * CHUNK, CHUNK), CHUNK)

    def peer(k):
        return lax.rem(view + k, views)

    def remote(src, dst, send, recv, device):
        return pltpu.make_async_remote_copy(
            src_ref=src, dst_ref=dst, send_sem=send, recv_sem=recv,
            device_id=device, device_id_type=MESH,
        )

    def halo_up(c):
        return remote(
            rounded.at[slab - HALF:slab, ys(c)], from_low.at[slab - HALF:slab, ys(c)],
            halo_send.at[0, c], halo_recv.at[0, c], {"tile": tile + 1},
        )

    def halo_down(c):
        return remote(
            rounded.at[0:HALF, ys(c)], from_high.at[0:HALF, ys(c)],
            halo_send.at[1, c], halo_recv.at[1, c], {"tile": tile - 1},
        )

    def mix(k, c):
        return remote(
            mixed.at[peer(k), :, ys(c)], first.at[:, ys(c, view * quarter)],
            mix_send.at[k - 1, c], mix_recv.at[k - 1, c], {"view": peer(k)},
        )

    def part(k, c):
        return remote(
            second.at[:, ys(c, peer(k) * quarter)], parts.at[view, :, ys(c)],
            part_send.at[k - 1, c], part_recv.at[k - 1, c], {"view": peer(k)},
        )

    def early(k, g):
        some = pl.ds(g * PLANES, PLANES)
        return remote(
            second.at[some, ys(0, peer(k) * quarter)], parts.at[view, some, ys(0)],
            early_send.at[k - 1, g], early_recv.at[k - 1, g], {"view": peer(k)},
        )

    groups = slab // PLANES

    def sum_up(c):
        return remote(
            to_high.at[:, ys(c)], back_low.at[:, ys(c)],
            sum_send.at[0, c], sum_recv.at[0, c], {"tile": tile + 1},
        )

    def sum_down(c):
        return remote(
            to_low.at[:, ys(c)], back_high.at[:, ys(c)],
            sum_send.at[1, c], sum_recv.at[1, c], {"tile": tile - 1},
        )

    def each_chunk(body):
        def step(c, carry):
            body(c)
            return carry
        lax.fori_loop(0, chunks, step, 0)

    rec_copy = pltpu.make_async_copy(recorded_hbm.at[0], recorded, rec_sem)
    rec_copy.start()
    for ref in (from_low, from_high, back_low, back_high):
        ref[...] = jnp.zeros_like(ref)
    barrier = pltpu.get_barrier_semaphore()
    for k in range(1, views):
        pl.semaphore_signal(barrier, inc=1, device_id={"view": peer(k)}, device_id_type=MESH)

    @pl.when(has_low)
    def _():
        pl.semaphore_signal(barrier, inc=1, device_id={"tile": tile - 1}, device_id_type=MESH)

    @pl.when(has_high)
    def _():
        pl.semaphore_signal(barrier, inc=1, device_id={"tile": tile + 1}, device_id_type=MESH)

    pl.semaphore_wait(
        barrier, views - 1 + has_low.astype(jnp.int32) + has_high.astype(jnp.int32)
    )

    def start_halo(c):
        @pl.when(has_high)
        def _():
            halo_up(c).start()

        @pl.when(has_low)
        def _():
            halo_down(c).start()

    start_halo(0)

    taps[...] = jnp.zeros_like(taps)
    rows, cols = slab * GROUP, 3 * slab * GROUP
    tap = lax.broadcasted_iota(jnp.int32, (taps.shape[1], cols), 0)
    spot = lax.broadcasted_iota(jnp.int32, (taps.shape[1], cols), 1)
    spread = ((spot == GROUP * (tap + slab - HALF)) & (tap < TAPS)).astype(F32).astype(BF16)
    for s in range(views):
        lines = picked_taps(assign_ref[s], half_ref, psf_ref, taps)
        line = dot(lines.astype(BF16), spread)[0:1]
        block = pltpu.roll(jnp.broadcast_to(line, (rows, cols)), 0, 1, stride=1, stride_axis=0)
        wide_a[s * rows:(s + 1) * rows, :] = block.astype(BF16)
        wide_b[:, s * rows:(s + 1) * rows] = block.T.astype(BF16)
    lines = picked_taps(assign_ref[view], half_ref, psf_ref, taps)
    totals = jnp.sum(lines, axis=1, keepdims=True)
    scale = 1.0 / (totals[0:1] * totals[1:2] * totals[2:3])
    across = band(lines[1:2], cy.shape[0])
    cy[...] = across.astype(BF16)
    cyt[...] = across.T.astype(BF16)
    cz[...] = band(lines[2:3], depth).astype(BF16)

    def blur_first(c):
        @pl.when(has_low)
        def _():
            halo_up(c).wait_recv()

        @pl.when(has_high)
        def _():
            halo_down(c).wait_recv()

        @pl.when(c + 1 < chunks)
        def _():
            start_halo(c + 1)

        cells = jnp.concatenate(
            [from_low[:, ys(c), :], rounded[:, ys(c), :], from_high[:, ys(c), :]], axis=0
        ).astype(F32)
        halves = []
        for h in range(0, CHUNK, GROUP):
            some = cells[:, h:h + GROUP, :].reshape(cols, depth).astype(BF16)
            halves.append(dot(wide_a[...], some).reshape(views * slab, GROUP, depth))
        mixed[:, :, ys(c), :] = (
            jnp.concatenate(halves, axis=1).astype(BF16).reshape(views, slab, CHUNK, depth)
        )
        for k in range(1, views):
            mix(k, c).start()
        first[:, ys(c, view * quarter), :] = mixed[view, :, ys(c), :]

    each_chunk(blur_first)

    def wait_mix(c):
        for k in range(1, views):
            mix(k, c).wait_recv()

    each_chunk(wait_mix)
    rec_copy.wait()

    def plane(i):
        blurred = dot(cy[...], first[i]).astype(BF16)
        blurred = dot_nt(blurred, cz[...]) * scale
        ratio = (recorded[i].astype(F32) / blurred).astype(BF16)
        back = dot(cyt[...], ratio).astype(BF16)
        second[i] = (dot(back, cz[...]) * scale).astype(BF16)

    def plane_group(g, carry):
        for i in range(PLANES):
            plane(g * PLANES + i)
        for k in range(1, views):
            early(k, g).start()
        return carry

    lax.fori_loop(0, groups, plane_group, 0)

    def start_parts(c, carry):
        for k in range(1, views):
            part(k, c).start()
        return carry

    lax.fori_loop(1, chunks, start_parts, 0)

    def wait_early(g, carry):
        for k in range(1, views):
            early(k, g).wait_recv()
        return carry

    def blur_last(c):
        @pl.when(c == 0)
        def _():
            lax.fori_loop(0, groups, wait_early, 0)

        @pl.when(c > 0)
        def _():
            for k in range(1, views):
                part(k, c).wait_recv()

        parts[view, :, ys(c), :] = second[:, ys(c, view * quarter), :]
        cells = parts[:, :, ys(c), :].astype(F32).reshape(views * slab, CHUNK, depth)
        halves = []
        for h in range(0, CHUNK, GROUP):
            some = cells[:, h:h + GROUP, :].reshape(views * rows, depth).astype(BF16)
            halves.append(dot(wide_b[...], some).reshape(3 * slab, GROUP, depth))
        wide = jnp.concatenate(halves, axis=1)
        out[:, ys(c), :] = wide[slab:2 * slab]
        for block, target, spare in (
            (wide[:slab], to_low, 0), (wide[2 * slab:], to_high, slab - 1)
        ):
            mean = (jnp.sum(block, axis=1) * (1.0 / CHUNK)).astype(BF16)
            target[:, ys(c), :] = (block - mean.astype(F32)[:, None, :]).astype(BF16)
            target[spare, ys(c), :] = mean

        @pl.when(has_high)
        def _():
            sum_up(c).start()

        @pl.when(has_low)
        def _():
            sum_down(c).start()

    each_chunk(blur_last)

    def add_sums(c):
        @pl.when(has_low)
        def _():
            sum_up(c).wait_recv()

        @pl.when(has_high)
        def _():
            sum_down(c).wait_recv()

        for came, spare in ((back_low, slab - 1), (back_high, 0)):
            mean = came[spare, ys(c), :].astype(F32)[:, None, :]
            added = came[:, ys(c), :].astype(F32) + mean
            for i in range(slab):
                if i != spare:
                    out[i, ys(c), :] += added[i]

    each_chunk(add_sums)

    def wait_sends(c):
        for k in range(1, views):
            mix(k, c).wait_send()

        @pl.when(c > 0)
        def _():
            for k in range(1, views):
                part(k, c).wait_send()

        @pl.when(has_high)
        def _():
            halo_up(c).wait_send()
            sum_up(c).wait_send()

        @pl.when(has_low)
        def _():
            halo_down(c).wait_send()
            sum_down(c).wait_send()

    each_chunk(wait_sends)

    def wait_early_sends(g, carry):
        for k in range(1, views):
            early(k, g).wait_send()
        return carry

    lax.fori_loop(0, groups, wait_early_sends, 0)


def shards(recorded, estimate, psf_taps, half_width, assign, flags):
    views = lax.axis_size("view")
    slab, quarter, depth = estimate.shape
    full_y = recorded.shape[2]
    chunks = quarter // CHUNK
    rows, cols = slab * GROUP, 3 * slab * GROUP
    cells = jnp.repeat(jnp.repeat(flags, 8, axis=0), 8, axis=1)[:, :, None] > 0
    vmem = pl.BlockSpec(memory_space=pltpu.VMEM)
    smem = pl.BlockSpec(memory_space=pltpu.SMEM)
    dma = pltpu.SemaphoreType.DMA
    edge = pltpu.VMEM((slab, quarter, depth), BF16)
    whole = pltpu.VMEM((slab, full_y, depth), BF16)
    total = pl.pallas_call(
        kernel,
        out_shape=jax.ShapeDtypeStruct(estimate.shape, F32),
        in_specs=[smem, smem, vmem, vmem, pl.BlockSpec(memory_space=pl.ANY)],
        out_specs=vmem,
        scratch_shapes=[
            pltpu.VMEM((8, 256), F32),
            pltpu.VMEM((views * rows, cols), BF16),
            pltpu.VMEM((cols, views * rows), BF16),
            pltpu.VMEM((full_y, full_y), BF16),
            pltpu.VMEM((full_y, full_y), BF16),
            pltpu.VMEM((depth, depth), BF16),
            whole,
            edge, edge,
            pltpu.VMEM((views, slab, quarter, depth), BF16),
            whole, whole,
            pltpu.VMEM((views, slab, quarter, depth), BF16),
            edge, edge, edge, edge,
            dma,
            dma((2, chunks)), dma((2, chunks)),
            dma((views - 1, chunks)), dma((views - 1, chunks)),
            dma((views - 1, chunks)), dma((views - 1, chunks)),
            dma((views - 1, slab // PLANES)), dma((views - 1, slab // PLANES)),
            dma((2, chunks)), dma((2, chunks)),
        ],
        compiler_params=pltpu.CompilerParams(collective_id=0, has_side_effects=True),
        name="deconvolve",
    )(assign, half_width.T, psf_taps.transpose(1, 0, 2), estimate.astype(BF16), recorded)
    return jnp.where(cells, estimate * (total / views), estimate)


def solution(mesh):
    placed = (
        P("view", "tile", None, None),
        P("tile", "view", None),
        P(),
        P(),
        P(),
        P("tile", "view"),
    )
    return jax.shard_map(
        shards, mesh=mesh, in_specs=placed, out_specs=P("tile", "view", None), check_vma=False
    )
```

```python
import jax
import jax.numpy as jnp
from jax import lax
from jax.experimental import pallas as pl
from jax.experimental.pallas import tpu as pltpu
from jax.sharding import PartitionSpec as P

TAPS = 31
HALF = TAPS // 2
GROUP = 8
CHUNK = 16
PLANES = 4
LANES = 128
STAGGER = 1
F32 = jnp.float32
BF16 = jnp.bfloat16
MESH = pl.DeviceIdType.MESH


def dot(a, b):
    return jnp.dot(a, b, preferred_element_type=F32)


def dot_nt(a, b):
    return lax.dot_general(a, b, (((1,), (1,)), ((), ())), preferred_element_type=F32)


def picked_taps(entry, half_ref, psf_ref, taps):
    for d in range(3):
        taps[d:d + 1, 0:TAPS] = psf_ref[d, pl.ds(entry, 1), :]
    row = lax.broadcasted_iota(jnp.int32, taps.shape, 0)
    col = lax.broadcasted_iota(jnp.int32, taps.shape, 1)
    width = jnp.where(
        row == 0, half_ref[0, entry], jnp.where(row == 1, half_ref[1, entry], half_ref[2, entry])
    )
    keep = (jnp.abs(col - HALF) <= width) & (col < TAPS) & (row < 3)
    return jnp.where(keep, taps[...], 0.0).astype(BF16).astype(F32)


def band(line, size):
    rolled = pltpu.roll(
        jnp.broadcast_to(line, (size, size)), size - HALF, 1, stride=1, stride_axis=0
    )
    row = lax.broadcasted_iota(jnp.int32, (size, size), 0)
    col = lax.broadcasted_iota(jnp.int32, (size, size), 1)
    return jnp.where(jnp.abs(row - col) <= HALF, rolled, 0.0)


def kernel(
    assign_ref, half_ref, psf_ref, estimate, recorded_hbm, out,
    rounded, taps, wide_a, wide_b, cy, cyt, cz, recorded,
    from_low, from_high, mixed, first, second, parts,
    to_low, to_high, back_low, back_high,
    rec_sem, halo_send, halo_recv, mix_send, mix_recv,
    part_send, part_recv, early_send, early_recv, sum_send, sum_recv,
):
    views = parts.shape[0]
    slab, quarter, depth = rounded.shape
    halves = depth // LANES
    pieces = (quarter // CHUNK) * halves
    tile, view = lax.axis_index("tile"), lax.axis_index("view")
    last = lax.axis_size("tile") - 1
    has_low, has_high = tile > 0, tile < last

    def ys(c, base=0):
        return pl.ds(pl.multiple_of(base + lax.div(c, halves) * CHUNK, CHUNK), CHUNK)

    def zs(c):
        return pl.ds(pl.multiple_of(lax.rem(c, halves) * LANES, LANES), LANES)

    def peer(k):
        return lax.rem(view + k, views)

    def remote(src, dst, send, recv, device):
        return pltpu.make_async_remote_copy(
            src_ref=src, dst_ref=dst, send_sem=send, recv_sem=recv,
            device_id=device, device_id_type=MESH,
        )

    def halo_up(c):
        return remote(
            rounded.at[slab - HALF:slab, ys(c), zs(c)], from_low.at[slab - HALF:slab, ys(c), zs(c)],
            halo_send.at[0, c], halo_recv.at[0, c], {"tile": tile + 1},
        )

    def halo_down(c):
        return remote(
            rounded.at[0:HALF, ys(c), zs(c)], from_high.at[0:HALF, ys(c), zs(c)],
            halo_send.at[1, c], halo_recv.at[1, c], {"tile": tile - 1},
        )

    def mix(k, c):
        return remote(
            mixed.at[peer(k), :, ys(c), zs(c)], first.at[:, ys(c, view * quarter), zs(c)],
            mix_send.at[k - 1, c], mix_recv.at[k - 1, c], {"view": peer(k)},
        )

    def part(k, c):
        return remote(
            second.at[:, ys(c, peer(k) * quarter), zs(c)], parts.at[view, :, ys(c), zs(c)],
            part_send.at[k - 1, c], part_recv.at[k - 1, c], {"view": peer(k)},
        )

    def early(k, g):
        some = pl.ds(g * PLANES, PLANES)
        return remote(
            second.at[some, ys(0, peer(k) * quarter)], parts.at[view, some, ys(0)],
            early_send.at[k - 1, g], early_recv.at[k - 1, g], {"view": peer(k)},
        )

    groups = slab // PLANES

    def sum_up(c):
        return remote(
            to_high.at[:, ys(c), zs(c)], back_low.at[:, ys(c), zs(c)],
            sum_send.at[0, c], sum_recv.at[0, c], {"tile": tile + 1},
        )

    def sum_down(c):
        return remote(
            to_low.at[:, ys(c), zs(c)], back_high.at[:, ys(c), zs(c)],
            sum_send.at[1, c], sum_recv.at[1, c], {"tile": tile - 1},
        )

    def each_chunk(body):
        def step(c, carry):
            body(c)
            return carry
        lax.fori_loop(0, pieces, step, 0)

    rec_copy = pltpu.make_async_copy(recorded_hbm.at[0], recorded, rec_sem)
    rec_copy.start()
    rounded[...] = estimate[...].astype(BF16)
    for ref in (from_low, from_high, back_low, back_high):
        ref[...] = jnp.zeros_like(ref)
    barrier = pltpu.get_barrier_semaphore()
    for k in range(1, views):
        pl.semaphore_signal(barrier, inc=1, device_id={"view": peer(k)}, device_id_type=MESH)

    @pl.when(has_low)
    def _():
        pl.semaphore_signal(barrier, inc=1, device_id={"tile": tile - 1}, device_id_type=MESH)

    @pl.when(has_high)
    def _():
        pl.semaphore_signal(barrier, inc=1, device_id={"tile": tile + 1}, device_id_type=MESH)

    pl.semaphore_wait(
        barrier, views - 1 + has_low.astype(jnp.int32) + has_high.astype(jnp.int32)
    )

    def start_halo(c):
        @pl.when(has_high)
        def _():
            halo_up(c).start()

        @pl.when(has_low)
        def _():
            halo_down(c).start()

    start_halo(0)

    taps[...] = jnp.zeros_like(taps)
    rows, cols = slab * GROUP, 3 * slab * GROUP
    tap = lax.broadcasted_iota(jnp.int32, (taps.shape[1], cols), 0)
    spot = lax.broadcasted_iota(jnp.int32, (taps.shape[1], cols), 1)
    spread = ((spot == GROUP * (tap + slab - HALF)) & (tap < TAPS)).astype(F32).astype(BF16)
    for s in range(views):
        lines = picked_taps(assign_ref[s], half_ref, psf_ref, taps)
        line = dot(lines.astype(BF16), spread)[0:1]
        block = pltpu.roll(jnp.broadcast_to(line, (rows, cols)), 0, 1, stride=1, stride_axis=0)
        wide_a[s * rows:(s + 1) * rows, :] = block.astype(BF16)
        wide_b[:, s * rows:(s + 1) * rows] = block.T.astype(BF16)
        if s == STAGGER:
            start_halo(1)
    lines = picked_taps(assign_ref[view], half_ref, psf_ref, taps)
    totals = jnp.sum(lines, axis=1, keepdims=True)
    scale = 1.0 / (totals[0:1] * totals[1:2] * totals[2:3])
    across = band(lines[1:2], cy.shape[0])
    cy[...] = across.astype(BF16)
    cyt[...] = across.T.astype(BF16)
    cz[...] = band(lines[2:3], depth).astype(BF16)

    def blur_first(c):
        @pl.when(has_low)
        def _():
            halo_up(c).wait_recv()

        @pl.when(has_high)
        def _():
            halo_down(c).wait_recv()

        @pl.when(c + 2 < pieces)
        def _():
            start_halo(c + 2)

        cells = jnp.concatenate(
            [from_low[:, ys(c), zs(c)], rounded[:, ys(c), zs(c)], from_high[:, ys(c), zs(c)]], axis=0
        ).astype(F32)
        blurs = []
        for h in range(0, CHUNK, GROUP):
            some = cells[:, h:h + GROUP, :].reshape(cols, LANES).astype(BF16)
            blurs.append(dot(wide_a[...], some).reshape(views * slab, GROUP, LANES))
        mixed[:, :, ys(c), zs(c)] = (
            jnp.concatenate(blurs, axis=1).astype(BF16).reshape(views, slab, CHUNK, LANES)
        )
        for k in range(1, views):
            mix(k, c).start()
        first[:, ys(c, view * quarter), zs(c)] = mixed[view, :, ys(c), zs(c)]

    each_chunk(blur_first)

    def wait_mix(c):
        for k in range(1, views):
            mix(k, c).wait_recv()

    each_chunk(wait_mix)
    rec_copy.wait()

    def plane(i):
        blurred = dot(cy[...], first[i]).astype(BF16)
        blurred = dot_nt(blurred, cz[...]) * scale
        ratio = (recorded[i].astype(F32) / blurred).astype(BF16)
        back = dot(cyt[...], ratio).astype(BF16)
        second[i] = (dot(back, cz[...]) * scale).astype(BF16)

    def plane_group(g, carry):
        for i in range(PLANES):
            plane(g * PLANES + i)
        for k in range(1, views):
            early(k, g).start()
        return carry

    lax.fori_loop(0, groups, plane_group, 0)

    def start_parts(c, carry):
        for k in range(1, views):
            part(k, c).start()
        return carry

    lax.fori_loop(halves, pieces, start_parts, 0)

    def wait_early(g, carry):
        for k in range(1, views):
            early(k, g).wait_recv()
        return carry

    def blur_last(c):
        @pl.when(c == 0)
        def _():
            lax.fori_loop(0, groups, wait_early, 0)

        @pl.when(c >= halves)
        def _():
            for k in range(1, views):
                part(k, c).wait_recv()

        parts[view, :, ys(c), zs(c)] = second[:, ys(c, view * quarter), zs(c)]
        cells = parts[:, :, ys(c), zs(c)].astype(F32).reshape(views * slab, CHUNK, LANES)
        blurs = []
        for h in range(0, CHUNK, GROUP):
            some = cells[:, h:h + GROUP, :].reshape(views * rows, LANES).astype(BF16)
            blurs.append(dot(wide_b[...], some).reshape(3 * slab, GROUP, LANES))
        wide = jnp.concatenate(blurs, axis=1)
        out[:, ys(c), zs(c)] = wide[slab:2 * slab]
        for block, target, spare in (
            (wide[:slab], to_low, 0), (wide[2 * slab:], to_high, slab - 1)
        ):
            mean = (jnp.sum(block, axis=1) * (1.0 / CHUNK)).astype(BF16)
            target[:, ys(c), zs(c)] = (block - mean.astype(F32)[:, None, :]).astype(BF16)
            target[spare, ys(c), zs(c)] = mean

        @pl.when(has_high)
        def _():
            sum_up(c).start()

        @pl.when(has_low)
        def _():
            sum_down(c).start()

    each_chunk(blur_last)

    def add_sums(c):
        @pl.when(has_low)
        def _():
            sum_up(c).wait_recv()

        @pl.when(has_high)
        def _():
            sum_down(c).wait_recv()

        for came, spare in ((back_low, slab - 1), (back_high, 0)):
            mean = came[spare, ys(c), zs(c)].astype(F32)[:, None, :]
            added = came[:, ys(c), zs(c)].astype(F32) + mean
            for i in range(slab):
                if i != spare:
                    out[i, ys(c), zs(c)] += added[i]

    each_chunk(add_sums)

    def wait_sends(c):
        for k in range(1, views):
            mix(k, c).wait_send()

        @pl.when(c >= halves)
        def _():
            for k in range(1, views):
                part(k, c).wait_send()

        @pl.when(has_high)
        def _():
            halo_up(c).wait_send()
            sum_up(c).wait_send()

        @pl.when(has_low)
        def _():
            halo_down(c).wait_send()
            sum_down(c).wait_send()

    each_chunk(wait_sends)

    def wait_early_sends(g, carry):
        for k in range(1, views):
            early(k, g).wait_send()
        return carry

    lax.fori_loop(0, groups, wait_early_sends, 0)


def shards(recorded, estimate, psf_taps, half_width, assign, flags):
    views = lax.axis_size("view")
    slab, quarter, depth = estimate.shape
    full_y = recorded.shape[2]
    chunks = (quarter // CHUNK) * (depth // LANES)
    rows, cols = slab * GROUP, 3 * slab * GROUP
    cells = jnp.repeat(jnp.repeat(flags, 8, axis=0), 8, axis=1)[:, :, None] > 0
    vmem = pl.BlockSpec(memory_space=pltpu.VMEM)
    smem = pl.BlockSpec(memory_space=pltpu.SMEM)
    dma = pltpu.SemaphoreType.DMA
    edge = pltpu.VMEM((slab, quarter, depth), BF16)
    whole = pltpu.VMEM((slab, full_y, depth), BF16)
    total = pl.pallas_call(
        kernel,
        out_shape=jax.ShapeDtypeStruct(estimate.shape, F32),
        in_specs=[smem, smem, vmem, vmem, pl.BlockSpec(memory_space=pl.ANY)],
        out_specs=vmem,
        scratch_shapes=[
            edge,
            pltpu.VMEM((8, 256), F32),
            pltpu.VMEM((views * rows, cols), BF16),
            pltpu.VMEM((cols, views * rows), BF16),
            pltpu.VMEM((full_y, full_y), BF16),
            pltpu.VMEM((full_y, full_y), BF16),
            pltpu.VMEM((depth, depth), BF16),
            whole,
            edge, edge,
            pltpu.VMEM((views, slab, quarter, depth), BF16),
            whole, whole,
            pltpu.VMEM((views, slab, quarter, depth), BF16),
            edge, edge, edge, edge,
            dma,
            dma((2, chunks)), dma((2, chunks)),
            dma((views - 1, chunks)), dma((views - 1, chunks)),
            dma((views - 1, chunks)), dma((views - 1, chunks)),
            dma((views - 1, slab // PLANES)), dma((views - 1, slab // PLANES)),
            dma((2, chunks)), dma((2, chunks)),
        ],
        compiler_params=pltpu.CompilerParams(collective_id=0, has_side_effects=True),
        name="deconvolve",
    )(assign, half_width.T, psf_taps.transpose(1, 0, 2), estimate, recorded)
    return jnp.where(cells, estimate * (total / views), estimate)


def solution(mesh):
    placed = (
        P("view", "tile", None, None),
        P("tile", "view", None),
        P(),
        P(),
        P(),
        P("tile", "view"),
    )
    return jax.shard_map(
        shards, mesh=mesh, in_specs=placed, out_specs=P("tile", "view", None), check_vma=False
    )
```
